32 devices in a mesh: strip: 8 (over z, core), basis: 4 (over y, x).
Axes of the slice: x: 2, y: 2, z: 4, core: 2. Of those that a mesh axis runs over, the one named last changes fastest.
Arguments:
- sky_image: float32 [1024, 1024], P('strip', 'basis'), may hold values from -6 to 6
- dual_coeffs: float32 [8, 1024, 1024], P('basis', 'strip'), may hold values from -2 to 2
- thresholds: float32 [8, 1024, 1024], P('basis', 'strip'), may hold values from 0.05 to 1
Outputs:
- dual_next: float32 [8, 1024, 1024], P('basis', 'strip')
- adjoint_image: float32 [1024, 1024], P('strip', 'basis')
The draws below stay inside these ranges and needn't reach their ends.
All inputs are finite; a program needn't handle non-finite values.
Results may differ from the reference program's by a relative error of at most 0.00002.
Values sent between devices are 32-bit elements; how exact they have to be, the bound alone decides.
A program may use at most 64 MiB of HBM per device.

```python
import math
import jax
import jax.numpy as jnp
import numpy as np

COLS = 1024
BASES = 8
LEVELS = 3
NX = 1024


def shard_levels(rng, extent, pieces, smallest, largest):
    loudness = 1.0
    for axis_at, parts in pieces:
        draws = jax.random.uniform(jax.random.fold_in(jax.random.fold_in(rng, 6), axis_at), (parts,), jnp.float32, smallest / len(pieces), largest / len(pieces))
        loudness = loudness * jnp.repeat(jnp.exp(draws), extent[axis_at] // parts).reshape((-1,) + (1,) * (len(extent) - 1 - axis_at))
    return loudness


def scatter_about(stream_key, shape, spread, reach, cuts=(), kind=jnp.bfloat16):
    loudness = shard_levels(stream_key, shape, cuts, -0.22, 0.18) if cuts else 1.0
    drawn = jax.random.normal(stream_key, shape, jnp.float32) * spread * loudness
    return jnp.minimum(jnp.maximum(drawn, -reach), reach).astype(kind)


def setup_inputs(seed: int = 0) -> dict:
    keys = jax.random.split(jax.random.key(seed), 4)
    return {
        "sky_image": scatter_about(keys[0], (NX, COLS), 1.0, 6.0, ((0, 8), (1, 4)), jnp.float32),
        "dual_coeffs": scatter_about(keys[1], (BASES, NX, COLS), 0.3, 2.0, ((0, 4), (1, 8)), jnp.float32),
        "thresholds": jnp.clip(jnp.exp(math.log(1.0) - 2.9957323 * jax.random.uniform(keys[2], (BASES, NX, COLS), jnp.float32) ** shard_levels(keys[2], (BASES, NX, COLS), ((0, 4), (1, 8)), -0.2, 0.2)), 0.05, 1.0),
    }


daubechies = [[0.7071067811865476, 0.7071067811865476], [0.48296291314469025, 0.836516303737469, 0.22414386804185735, -0.12940952255092145], [0.3326705529509569, 0.8068915093133388, 0.4598775021193313, -0.13501102001039084, -0.08544127388224149, 0.035226291882100656], [0.23037781330885523, 0.7148465705525415, 0.6308807679295904, -0.02798376941698385, -0.18703481171888114, 0.030841381835986965, 0.032883011666982945, -0.010597401784997278], [0.160102397974125, 0.6038292697974729, 0.7243085284385744, 0.13842814590110342, -0.24229488706619015, -0.03224486958502952, 0.07757149384006515, -0.006241490213011705, -0.012580751999015526, 0.003335725285001549], [0.11154074335008017, 0.4946238903983854, 0.7511339080215775, 0.3152503517092432, -0.22626469396516913, -0.12976686756709563, 0.09750160558707936, 0.02752286553001629, -0.031582039318031156, 0.0005538422009938016, 0.004777257511010651, -0.00107730108499558], [0.07785205408506236, 0.39653931948230575, 0.7291320908465551, 0.4697822874053586, -0.14390600392910627, -0.22403618499416572, 0.07130921926705004, 0.08061260915106681, -0.03802993693503463, -0.01657454163101562, 0.012550998556013784, 0.00042957797300470274, -0.0018016407039998328, 0.0003537138000010399], [0.05441584224308161, 0.3128715909144659, 0.6756307362980128, 0.5853546836548691, -0.015829105256023893, -0.2840155429624281, 0.00047248457399797254, 0.128747426620186, -0.01736930100202211, -0.04408825393106472, 0.013981027917015516, 0.008746094047015655, -0.00487035299301066, -0.0003917403729959771, 0.0006754494059985568, -0.00011747678400228192]]

def filter_table():
    low_rows = np.zeros((8, 16), np.float32)
    high_rows = np.zeros((8, 16), np.float32)
    for basis_row, filter_taps in enumerate(daubechies):
        length = len(filter_taps)
        for tap_index in range(length):
            low_rows[basis_row, tap_index] = filter_taps[tap_index]
            high_rows[basis_row, tap_index] = (-1) ** tap_index * filter_taps[length - 1 - tap_index]
    return (low_rows, high_rows)

def weave(first_part, second_part, band_axis):
    stacked = jnp.stack((first_part, second_part), axis=band_axis)
    if band_axis == -2:
        new_shape = first_part.shape[:-2] + (2 * first_part.shape[-2], first_part.shape[-1])
    else:
        new_shape = first_part.shape[:-1] + (2 * first_part.shape[-1],)
    return stacked.reshape(new_shape)

def phase_part(signal, offset, band_axis):
    if band_axis == -2:
        return signal[..., offset::2, :]
    return signal[..., offset::2]

def split_axis(signal, low_pass, high_pass, band_axis):
    even_part = phase_part(signal, 0, band_axis)
    odd_part = phase_part(signal, 1, band_axis)
    for tap_pair in range(8):
        even_roll = jnp.roll(even_part, -tap_pair, axis=band_axis)
        odd_roll = jnp.roll(odd_part, -tap_pair, axis=band_axis)
        low_term = low_pass[2 * tap_pair] * even_roll + low_pass[2 * tap_pair + 1] * odd_roll
        high_term = high_pass[2 * tap_pair] * even_roll + high_pass[2 * tap_pair + 1] * odd_roll
        if tap_pair == 0:
            low_band, high_band = (low_term, high_term)
        else:
            low_band, high_band = (low_band + low_term, high_band + high_term)
    return (low_band, high_band)

def merge_axis(low_band, high_band, low_pass, high_pass, band_axis):
    for tap_pair in range(8):
        low_roll = jnp.roll(low_band, tap_pair, axis=band_axis)
        high_roll = jnp.roll(high_band, tap_pair, axis=band_axis)
        even_term = low_pass[2 * tap_pair] * low_roll + high_pass[2 * tap_pair] * high_roll
        odd_term = low_pass[2 * tap_pair + 1] * low_roll + high_pass[2 * tap_pair + 1] * high_roll
        if tap_pair == 0:
            even_sum, odd_sum = (even_term, odd_term)
        else:
            even_sum, odd_sum = (even_sum + even_term, odd_sum + odd_term)
    return weave(even_sum, odd_sum, band_axis)

def analyse(signal, low_pass, high_pass, levels_left):
    top_half, bottom = split_axis(signal, low_pass, high_pass, -2)
    coarse, band_lh = split_axis(top_half, low_pass, high_pass, -1)
    band_hl, band_hh = split_axis(bottom, low_pass, high_pass, -1)
    if levels_left > 1:
        coarse = analyse(coarse, low_pass, high_pass, levels_left - 1)
    return weave(weave(coarse, band_lh, -1), weave(band_hl, band_hh, -1), -2)

def synthesize(coefficients, low_pass, high_pass, levels_left):
    coarse = coefficients[..., 0::2, 0::2]
    band_lh = coefficients[..., 0::2, 1::2]
    band_hl = coefficients[..., 1::2, 0::2]
    band_hh = coefficients[..., 1::2, 1::2]
    if levels_left > 1:
        coarse = synthesize(coarse, low_pass, high_pass, levels_left - 1)
    top_half = merge_axis(coarse, band_lh, low_pass, high_pass, -1)
    bottom = merge_axis(band_hl, band_hh, low_pass, high_pass, -1)
    return merge_axis(top_half, bottom, low_pass, high_pass, -2)

def reference(sky_image, dual_coeffs, thresholds):
    low_rows, high_rows = filter_table()
    norm_scale = 1.0 / math.sqrt(BASES)
    updated_list = []
    summed = jnp.zeros(sky_image.shape, jnp.float32)
    for basis_index in range(BASES):
        low_pass = [float(low_rows[basis_index, tap_index]) for tap_index in range(16)]
        high_pass = [float(high_rows[basis_index, tap_index]) for tap_index in range(16)]
        coefficients = analyse(sky_image, low_pass, high_pass, LEVELS) * norm_scale
        updated = jnp.clip(dual_coeffs[basis_index] + coefficients, -thresholds[basis_index], thresholds[basis_index])
        updated_list.append(updated)
        summed = summed + synthesize(updated, low_pass, high_pass, LEVELS)
    return (jnp.stack(updated_list), summed * norm_scale)
```

```python
import functools
import math

import jax
import jax.numpy as jnp
import numpy as np
from jax import lax
from jax.experimental import pallas as pl
from jax.experimental.pallas import tpu as pltpu
from jax.sharding import PartitionSpec as P

BASES = 8
LEVELS = 3


daubechies = [
    [0.7071067811865476, 0.7071067811865476],
    [0.48296291314469025, 0.836516303737469, 0.22414386804185735, -0.12940952255092145],
    [
        0.3326705529509569,
        0.8068915093133388,
        0.4598775021193313,
        -0.13501102001039084,
        -0.08544127388224149,
        0.035226291882100656,
    ],
    [
        0.23037781330885523,
        0.7148465705525415,
        0.6308807679295904,
        -0.02798376941698385,
        -0.18703481171888114,
        0.030841381835986965,
        0.032883011666982945,
        -0.010597401784997278,
    ],
    [
        0.160102397974125,
        0.6038292697974729,
        0.7243085284385744,
        0.13842814590110342,
        -0.24229488706619015,
        -0.03224486958502952,
        0.07757149384006515,
        -0.006241490213011705,
        -0.012580751999015526,
        0.003335725285001549,
    ],
    [
        0.11154074335008017,
        0.4946238903983854,
        0.7511339080215775,
        0.3152503517092432,
        -0.22626469396516913,
        -0.12976686756709563,
        0.09750160558707936,
        0.02752286553001629,
        -0.031582039318031156,
        0.0005538422009938016,
        0.004777257511010651,
        -0.00107730108499558,
    ],
    [
        0.07785205408506236,
        0.39653931948230575,
        0.7291320908465551,
        0.4697822874053586,
        -0.14390600392910627,
        -0.22403618499416572,
        0.07130921926705004,
        0.08061260915106681,
        -0.03802993693503463,
        -0.01657454163101562,
        0.012550998556013784,
        0.00042957797300470274,
        -0.0018016407039998328,
        0.0003537138000010399,
    ],
    [
        0.05441584224308161,
        0.3128715909144659,
        0.6756307362980128,
        0.5853546836548691,
        -0.015829105256023893,
        -0.2840155429624281,
        0.00047248457399797254,
        0.128747426620186,
        -0.01736930100202211,
        -0.04408825393106472,
        0.013981027917015516,
        0.008746094047015655,
        -0.00487035299301066,
        -0.0003917403729959771,
        0.0006754494059985568,
        -0.00011747678400228192,
    ],
]


def filter_table():
    low_rows = np.zeros((8, 16), np.float32)
    high_rows = np.zeros((8, 16), np.float32)
    for basis_row, filter_taps in enumerate(daubechies):
        length = len(filter_taps)
        for tap_index in range(length):
            low_rows[basis_row, tap_index] = filter_taps[tap_index]
            high_rows[basis_row, tap_index] = (-1) ** tap_index * filter_taps[
                length - 1 - tap_index
            ]
    return (low_rows, high_rows)


def spread(taps, step):
    wide = np.zeros(((len(taps) - 1) * step + 1,), np.float64)
    wide[::step] = taps
    return wide


def level_table(tile):
    low_rows, high_rows = filter_table()
    table = np.zeros((low_rows.shape[0], 2 * tile, 2 * tile), np.float64)
    for basis in range(low_rows.shape[0]):
        count = 2 * (basis + 1)
        low = low_rows[basis, :count].astype(np.float64)
        high = high_rows[basis, :count].astype(np.float64)
        before, offset = np.ones((1,), np.float64), 0
        for level in range(LEVELS):
            step = 2**level
            low_comp = np.convolve(spread(low, step), before)
            high_comp = np.convolve(spread(high, step), before)
            for row in range(tile // step):
                start = (row // 2) * 2 * step
                comp = low_comp if row % 2 == 0 else high_comp
                table[basis, offset + row, start : start + len(comp)] = comp
            before, offset = low_comp, offset + tile // step
    halves = np.stack([table[:, :, :tile], table[:, :, tile:]], axis=1)
    return halves.astype(np.float32)


def bf16_pair(value):
    high = value.astype(jnp.bfloat16)
    return high, (value - high.astype(jnp.float32)).astype(jnp.bfloat16)


def dot(left, right):
    return lax.dot_general(
        left, right, (((1,), (0,)), ((), ())), preferred_element_type=jnp.float32
    )


def flip_bits(index, mask):
    flipped, bit = index, 1
    while bit <= mask:
        if mask & bit:
            flipped = flipped + bit - 2 * bit * ((index // bit) % 2)
        bit *= 2
    return flipped


def kernel(
    cfg, sky, table, dual, thresholds, out_dual, out_image,
    xg, tabv, wov, a_lhs, a_t, g_an, g_sy, dualv, thrv, z_hi, z_lo, coef, dtile, e_hi, e_lo,
    pbuf, hbuf, rbuf,
    load_sem, store_sem, bs_send, bs_recv, hs_send, hs_recv, rs_send, rs_recv, ps_send, ps_recv,
):
    n_strip, n_basis, bases, tile, width, cols, halo = cfg
    tiles, per_block = cols // tile, width // tile
    strip, me = lax.axis_index("strip"), lax.axis_index("basis")
    after, behind = lax.rem(strip + 1, n_strip), lax.rem(strip + n_strip - 1, n_strip)
    peers = [me] + [flip_bits(me, mask) for mask in range(1, n_basis)]
    norm_scale = 1.0 / math.sqrt(BASES)
    offsets = [0]
    for level in range(LEVELS):
        offsets.append(offsets[-1] + tile // 2**level)
    used = offsets[-1]

    loads = []
    table_copy = pltpu.make_async_copy(table.at[pl.ds(me * bases, bases)], tabv, load_sem.at[0])
    table_copy.start()
    for which, (src, dst) in enumerate(((dual, dualv), (thresholds, thrv))):
        for j in range(tiles):
            copy = pltpu.make_async_copy(
                src.at[:, :, pl.ds(j * tile, tile)], dst.at[:, j], load_sem.at[1 + which * tiles + j]
            )
            copy.start()
            loads.append(copy)

    barrier = pltpu.get_barrier_semaphore()
    for peer in peers[1:]:
        pl.semaphore_signal(barrier, inc=1, device_id=(strip, peer), device_id_type=pl.DeviceIdType.MESH)
    for other in (after, behind):
        pl.semaphore_signal(barrier, inc=1, device_id=(other, me), device_id_type=pl.DeviceIdType.MESH)
    pl.semaphore_wait(barrier, n_basis + 1)

    def remote(src, dst, send, recv, target):
        return pltpu.make_async_remote_copy(
            src_ref=src, dst_ref=dst, send_sem=send, recv_sem=recv,
            device_id=target, device_id_type=pl.DeviceIdType.MESH,
        )

    block_copies = [None]
    for d in range(1, n_basis):
        block_copies.append(
            remote(sky, xg.at[me, pl.ds(0, tile)], bs_send.at[d], bs_recv.at[d], (strip, peers[d]))
        )
    halo_copies = [
        remote(sky.at[pl.ds(0, halo)], xg.at[me, pl.ds(tile, halo)], hs_send.at[0], hs_recv.at[0], (behind, me))
    ]
    for d in range(1, n_basis):
        halo_copies.append(
            remote(
                xg.at[peers[d], pl.ds(0, halo)], xg.at[peers[d], pl.ds(tile, halo)],
                hs_send.at[d], hs_recv.at[d], (behind, me),
            )
        )
    halo_copies[0].start()
    for d in range(1, n_basis):
        block_copies[d].start()

    xg[me, 0:tile, :] = sky[...]
    if halo < tile:
        for d in range(n_basis):
            xg[d, tile + halo :, :] = jnp.zeros((tile - halo, width), jnp.float32)

    table_copy.wait()
    for b in range(bases):
        wov[...] = jnp.zeros_like(wov)
        for half in range(2):
            a_high, a_low = bf16_pair(tabv[b, half, :used])
            a_lhs[b, :used, half * tile : (half + 1) * tile] = a_high
            a_lhs[b, used:, half * tile : (half + 1) * tile] = a_low
            t_high, t_low = bf16_pair(tabv[b, half].T)
            a_t[half * tile : (half + 1) * tile, b * 2 * tile : (b + 1) * 2 * tile] = t_high
            a_t[(2 + half) * tile : (3 + half) * tile, b * 2 * tile : (b + 1) * 2 * tile] = t_low
            for level in range(LEVELS):
                rows = tabv[b, half, offsets[level] : offsets[level + 1]]
                if level > 0:
                    slot = wov.at[level - 1, half]
                    slot[pl.ds(0, tile // 2**level, stride=2**level), :] = rows
                    rows = slot[...]
                g_high, g_low = bf16_pair(rows)
                s = (1 - half) * tile
                g_sy[b, level, s : s + tile, :tile] = g_high
                g_sy[b, level, s : s + tile, tile:] = g_low
                g_high, g_low = bf16_pair(rows.T)
                s = half * tile
                g_an[b, level, s : s + tile, :tile] = g_high
                g_an[b, level, s : s + tile, tile:] = g_low

    for d in range(1, n_basis):
        block_copies[d].wait_recv()
        halo_copies[d].start()

    for d in range(n_basis):
        halo_copies[d].wait_recv()
        x_high, x_low = bf16_pair(xg[peers[d]])
        for b in range(bases):
            wide = dot(a_lhs[b], x_high)
            z = wide[:used] + wide[used:] + dot(a_lhs[b, :used], x_low)
            high, low = bf16_pair(z)
            for part in range(per_block):
                at = peers[d] * per_block + part
                z_hi[b, at, :, :] = high[:, part * tile : (part + 1) * tile]
                z_lo[b, at, :, :] = low[:, part * tile : (part + 1) * tile]

    for copy in loads:
        copy.wait()
    lane = lax.broadcasted_iota(jnp.int32, (tile, tile), 1)
    row = lax.broadcasted_iota(jnp.int32, (tile, tile), 0)
    stores = []

    def windows(source, first, last, step):
        pieces = [source(j)[first:last] for j in range(tiles)]
        return jnp.concatenate(
            [
                jnp.concatenate(
                    [pieces[j], pieces[(j + 1) % tiles]] if step > 0 else [pieces[j - 1], pieces[j]], axis=1
                )
                for j in range(tiles)
            ],
            axis=0,
        )

    def columns(high_src, low_src, matrix, first, last, step):
        wide = dot(windows(high_src, first, last, step), matrix[...])
        return wide[:, :tile] + wide[:, tile:] + dot(windows(low_src, first, last, step), matrix[:, :tile])

    for b in range(bases):
        for level in range(LEVELS):
            y = columns(
                lambda j: z_hi[b, j], lambda j: z_lo[b, j], g_an.at[b, level],
                offsets[level], offsets[level + 1], 1,
            )
            stride, many = 2**level, tile // 2**level
            for j in range(tiles):
                mine = y[j * many : (j + 1) * many]
                slot = coef.at[j]
                if level == 0:
                    slot[...] = mine
                else:
                    held = slot[pl.ds(0, many, stride=stride), :]
                    slot[pl.ds(0, many, stride=stride), :] = jnp.where(
                        lane[:many] % stride == 0, mine, held
                    )
        for j in range(tiles):
            limit = thrv[b, j]
            dtile[b, j, :, :] = jnp.clip(dualv[b, j] + coef[j] * norm_scale, -limit, limit)
            copy = pltpu.make_async_copy(
                dtile.at[b, j], out_dual.at[b, :, pl.ds(j * tile, tile)], store_sem.at[b * tiles + j]
            )
            copy.start()
            stores.append(copy)
        for level in range(LEVELS):
            stride, many = 2**level, tile // 2**level
            highs, lows = [], []
            for j in range(tiles):
                slot = dtile.at[b, j]
                value = slot[...] if level == 0 else slot[pl.ds(0, many, stride=stride), :]
                if level < LEVELS - 1:
                    deeper = (row[:many] % 2 == 0) & (lane[:many] % (2 * stride) == 0)
                    value = jnp.where(deeper, 0.0, value)
                high, low = bf16_pair(value)
                highs.append(high)
                lows.append(low)
            e = columns(lambda j: highs[j], lambda j: lows[j], g_sy.at[b, level], 0, many, -1)
            e_high, e_low = bf16_pair(e)
            first = b * 2 * tile + offsets[level]
            for j in range(tiles):
                e_hi[j, first : first + many, :] = e_high[j * many : (j + 1) * many]
                e_lo[j, first : first + many, :] = e_low[j * many : (j + 1) * many]
        first = b * 2 * tile + used
        rest = 2 * tile - used
        for j in range(tiles):
            e_hi[j, first : first + rest, :] = jnp.zeros((rest, tile), jnp.bfloat16)
            e_lo[j, first : first + rest, :] = jnp.zeros((rest, tile), jnp.bfloat16)

    order = list(range(n_basis - 1, -1, -1))
    carry_copies, part_copies = {}, {}
    for d in order:
        at = peers[d]
        e_h = jnp.concatenate([e_hi[at * per_block + part] for part in range(per_block)], axis=1)
        e_l = jnp.concatenate([e_lo[at * per_block + part] for part in range(per_block)], axis=1)
        wide = dot(a_t[...], e_h)
        pbuf[d, :, :] = wide[: 2 * tile] + wide[2 * tile :] + dot(a_t[: 2 * tile], e_l)
        carry_copies[d] = remote(
            pbuf.at[d, pl.ds(tile, halo)], hbuf.at[d], ps_send.at[d], ps_recv.at[d], (after, me)
        )
        carry_copies[d].start()
    for d in order:
        carry_copies[d].wait_recv()
        pbuf[d, :halo, :] = pbuf[d, :halo, :] + hbuf[d]
        if d > 0:
            part_copies[d] = remote(
                pbuf.at[d, pl.ds(0, tile)], rbuf.at[d], rs_send.at[d], rs_recv.at[d], (strip, peers[d])
            )
            part_copies[d].start()
    total = pbuf[0, :tile, :]
    for d in order:
        if d > 0:
            part_copies[d].wait_recv()
            total = total + rbuf[d]
    out_image[...] = total * norm_scale

    for d in range(n_basis):
        halo_copies[d].wait_send()
        carry_copies[d].wait_send()
        if d > 0:
            block_copies[d].wait_send()
            part_copies[d].wait_send()
    for copy in stores:
        copy.wait()


def solution(mesh):
    n_strip, n_basis = mesh.shape["strip"], mesh.shape["basis"]

    def on_device(sky_image, dual_coeffs, thresholds):
        bases, tile, cols = dual_coeffs.shape
        width = sky_image.shape[1]
        tiles = cols // tile
        reach = 2 * BASES - 2
        halo = -(-reach * (2**LEVELS - 1) // 8) * 8
        assert halo <= tile and width % tile == 0 and cols == width * n_basis
        assert n_basis & (n_basis - 1) == 0 and tile % 2**LEVELS == 0
        used = sum(tile // 2**level for level in range(LEVELS))
        f32, bf16 = jnp.float32, jnp.bfloat16
        dma = pltpu.SemaphoreType.DMA
        vmem, anywhere = pl.BlockSpec(memory_space=pltpu.VMEM), pl.BlockSpec(memory_space=pl.ANY)
        table = jnp.asarray(level_table(tile))
        return pl.pallas_call(
            functools.partial(kernel, (n_strip, n_basis, bases, tile, width, cols, halo)),
            out_shape=(
                jax.ShapeDtypeStruct(dual_coeffs.shape, f32),
                jax.ShapeDtypeStruct(sky_image.shape, f32),
            ),
            in_specs=[vmem, anywhere, anywhere, anywhere],
            out_specs=(anywhere, vmem),
            scratch_shapes=[
                pltpu.VMEM((n_basis, 2 * tile, width), f32),
                pltpu.VMEM((bases, 2, 2 * tile, tile), f32),
                pltpu.VMEM((LEVELS - 1, 2, tile, tile), f32),
                pltpu.VMEM((bases, 2 * used, 2 * tile), bf16),
                pltpu.VMEM((4 * tile, bases * 2 * tile), bf16),
                pltpu.VMEM((bases, LEVELS, 2 * tile, 2 * tile), bf16),
                pltpu.VMEM((bases, LEVELS, 2 * tile, 2 * tile), bf16),
                pltpu.VMEM((bases, tiles, tile, tile), f32),
                pltpu.VMEM((bases, tiles, tile, tile), f32),
                pltpu.VMEM((bases, tiles, used, tile), bf16),
                pltpu.VMEM((bases, tiles, used, tile), bf16),
                pltpu.VMEM((tiles, tile, tile), f32),
                pltpu.VMEM((bases, tiles, tile, tile), f32),
                pltpu.VMEM((tiles, bases * 2 * tile, tile), bf16),
                pltpu.VMEM((tiles, bases * 2 * tile, tile), bf16),
                pltpu.VMEM((n_basis, 2 * tile, width), f32),
                pltpu.VMEM((n_basis, halo, width), f32),
                pltpu.VMEM((n_basis, tile, width), f32),
                dma((1 + 2 * tiles,)),
                dma((bases * tiles,)),
            ] + [dma((n_basis,)) for _ in range(8)],
            compiler_params=pltpu.CompilerParams(
                collective_id=0, has_side_effects=True, vmem_limit_bytes=48 * 2**20
            ),
        )(sky_image, table, dual_coeffs, thresholds)

    placed = (P("strip", "basis"), P("basis", "strip", None), P("basis", "strip", None))
    return jax.shard_map(
        on_device,
        mesh=mesh,
        in_specs=placed,
        out_specs=(P("basis", "strip", None), P("strip", "basis")),
        check_vma=False,
    )
```

```python
import functools
import math

import jax
import jax.numpy as jnp
import numpy as np
from jax import lax
from jax.experimental import pallas as pl
from jax.experimental.pallas import tpu as pltpu
from jax.sharding import PartitionSpec as P

BASES = 8
LEVELS = 3


daubechies = [
    [0.7071067811865476, 0.7071067811865476],
    [0.48296291314469025, 0.836516303737469, 0.22414386804185735, -0.12940952255092145],
    [
        0.3326705529509569,
        0.8068915093133388,
        0.4598775021193313,
        -0.13501102001039084,
        -0.08544127388224149,
        0.035226291882100656,
    ],
    [
        0.23037781330885523,
        0.7148465705525415,
        0.6308807679295904,
        -0.02798376941698385,
        -0.18703481171888114,
        0.030841381835986965,
        0.032883011666982945,
        -0.010597401784997278,
    ],
    [
        0.160102397974125,
        0.6038292697974729,
        0.7243085284385744,
        0.13842814590110342,
        -0.24229488706619015,
        -0.03224486958502952,
        0.07757149384006515,
        -0.006241490213011705,
        -0.012580751999015526,
        0.003335725285001549,
    ],
    [
        0.11154074335008017,
        0.4946238903983854,
        0.7511339080215775,
        0.3152503517092432,
        -0.22626469396516913,
        -0.12976686756709563,
        0.09750160558707936,
        0.02752286553001629,
        -0.031582039318031156,
        0.0005538422009938016,
        0.004777257511010651,
        -0.00107730108499558,
    ],
    [
        0.07785205408506236,
        0.39653931948230575,
        0.7291320908465551,
        0.4697822874053586,
        -0.14390600392910627,
        -0.22403618499416572,
        0.07130921926705004,
        0.08061260915106681,
        -0.03802993693503463,
        -0.01657454163101562,
        0.012550998556013784,
        0.00042957797300470274,
        -0.0018016407039998328,
        0.0003537138000010399,
    ],
    [
        0.05441584224308161,
        0.3128715909144659,
        0.6756307362980128,
        0.5853546836548691,
        -0.015829105256023893,
        -0.2840155429624281,
        0.00047248457399797254,
        0.128747426620186,
        -0.01736930100202211,
        -0.04408825393106472,
        0.013981027917015516,
        0.008746094047015655,
        -0.00487035299301066,
        -0.0003917403729959771,
        0.0006754494059985568,
        -0.00011747678400228192,
    ],
]


def filter_table():
    low_rows = np.zeros((8, 16), np.float32)
    high_rows = np.zeros((8, 16), np.float32)
    for basis_row, filter_taps in enumerate(daubechies):
        length = len(filter_taps)
        for tap_index in range(length):
            low_rows[basis_row, tap_index] = filter_taps[tap_index]
            high_rows[basis_row, tap_index] = (-1) ** tap_index * filter_taps[
                length - 1 - tap_index
            ]
    return (low_rows, high_rows)


def spread(taps, step):
    wide = np.zeros(((len(taps) - 1) * step + 1,), np.float64)
    wide[::step] = taps
    return wide


def level_table(tile):
    low_rows, high_rows = filter_table()
    table = np.zeros((low_rows.shape[0], 2 * tile, 2 * tile), np.float64)
    for basis in range(low_rows.shape[0]):
        count = 2 * (basis + 1)
        low = low_rows[basis, :count].astype(np.float64)
        high = high_rows[basis, :count].astype(np.float64)
        before, offset = np.ones((1,), np.float64), 0
        for level in range(LEVELS):
            step = 2**level
            low_comp = np.convolve(spread(low, step), before)
            high_comp = np.convolve(spread(high, step), before)
            for row in range(tile // step):
                start = (row // 2) * 2 * step
                comp = low_comp if row % 2 == 0 else high_comp
                table[basis, offset + row, start : start + len(comp)] = comp
            before, offset = low_comp, offset + tile // step
    halves = np.stack([table[:, :, :tile], table[:, :, tile:]], axis=1)
    return halves.astype(np.float32)


def bf16_pair(value):
    high = value.astype(jnp.bfloat16)
    return high, (value - high.astype(jnp.float32)).astype(jnp.bfloat16)


def dot(left, right):
    return lax.dot_general(
        left, right, (((1,), (0,)), ((), ())), preferred_element_type=jnp.float32
    )


def flip_bits(index, mask):
    flipped, bit = index, 1
    while bit <= mask:
        if mask & bit:
            flipped = flipped + bit - 2 * bit * ((index // bit) % 2)
        bit *= 2
    return flipped


def kernel(
    cfg, sky, table, dual, thresholds, out_dual, out_image,
    xg, tabv, wov, a_lhs, a_t, g_an, g_sy, dualv, thrv, z_hi, z_lo, coef, dtile, e_hi, e_lo,
    pbuf, hbuf, rbuf,
    load_sem, store_sem, bs_send, bs_recv, hs_send, hs_recv, rs_send, rs_recv, ps_send, ps_recv,
):
    n_strip, n_basis, bases, tile, width, cols, halo = cfg
    tiles, per_block = cols // tile, width // tile
    strip, me = lax.axis_index("strip"), lax.axis_index("basis")
    after, behind = lax.rem(strip + 1, n_strip), lax.rem(strip + n_strip - 1, n_strip)
    peers = [me] + [flip_bits(me, mask) for mask in range(1, n_basis)]
    norm_scale = 1.0 / math.sqrt(BASES)
    offsets = [0]
    for level in range(LEVELS):
        offsets.append(offsets[-1] + tile // 2**level)
    used = offsets[-1]

    loads = []
    table_copy = pltpu.make_async_copy(table.at[pl.ds(me * bases, bases)], tabv, load_sem.at[0])
    table_copy.start()
    for which, (src, dst) in enumerate(((dual, dualv), (thresholds, thrv))):
        for j in range(tiles):
            copy = pltpu.make_async_copy(
                src.at[:, :, pl.ds(j * tile, tile)], dst.at[:, j], load_sem.at[1 + which * tiles + j]
            )
            copy.start()
            loads.append(copy)

    barrier = pltpu.get_barrier_semaphore()
    for peer in peers[1:]:
        pl.semaphore_signal(barrier, inc=1, device_id=(strip, peer), device_id_type=pl.DeviceIdType.MESH)
    for other in (after, behind):
        pl.semaphore_signal(barrier, inc=1, device_id=(other, me), device_id_type=pl.DeviceIdType.MESH)
    pl.semaphore_wait(barrier, n_basis + 1)

    def remote(src, dst, send, recv, target):
        return pltpu.make_async_remote_copy(
            src_ref=src, dst_ref=dst, send_sem=send, recv_sem=recv,
            device_id=target, device_id_type=pl.DeviceIdType.MESH,
        )

    halves = ((0, tile // 2), (tile // 2, tile // 2))
    halo_halves = [(first, min(count, halo - first)) for first, count in halves if halo > first]
    block_copies, halo_copies = {}, {}
    single = list(range(1, n_basis))
    for d in range(1, n_basis):
        for p, (first, count) in enumerate(halves):
            rows = pl.ds(first, count)
            if d in single:
                source, held, target = sky.at[rows], me, peers[d]
            else:
                bit = (d & -d) if p == 0 else 1 << (d.bit_length() - 1)
                held, target = peers[d ^ bit], peers[bit]
                source = xg.at[held, rows]
            block_copies[d, p] = remote(
                source, xg.at[held, rows], bs_send.at[d, p], bs_recv.at[d, p], (strip, target)
            )
    for d in range(n_basis):
        for p, (first, count) in enumerate(halo_halves):
            source = sky.at[pl.ds(first, count)] if d == 0 else xg.at[peers[d], pl.ds(first, count)]
            halo_copies[d, p] = remote(
                source, xg.at[peers[d], pl.ds(tile + first, count)],
                hs_send.at[d, p], hs_recv.at[d, p], (behind, me),
            )
    for p in range(2):
        for d in single:
            block_copies[d, 1 - p if d == 1 else p].start()
    for p in range(len(halo_halves)):
        halo_copies[0, p].start()
    own_copy = pltpu.make_async_copy(sky, xg.at[me, pl.ds(0, tile)], load_sem.at[1 + 2 * tiles])
    own_copy.start()

    if halo < tile:
        for d in range(n_basis):
            xg[d, tile + halo :, :] = jnp.zeros((tile - halo, width), jnp.float32)

    table_copy.wait()
    for b in range(bases):
        wov[...] = jnp.zeros_like(wov)
        for half in range(2):
            a_high, a_low = bf16_pair(tabv[b, half, :used])
            a_lhs[b, :used, half * tile : (half + 1) * tile] = a_high
            a_lhs[b, used:, half * tile : (half + 1) * tile] = a_low
            t_high, t_low = bf16_pair(tabv[b, half].T)
            a_t[half * tile : (half + 1) * tile, b * 2 * tile : (b + 1) * 2 * tile] = t_high
            a_t[(2 + half) * tile : (3 + half) * tile, b * 2 * tile : (b + 1) * 2 * tile] = t_low
            for level in range(LEVELS):
                rows = tabv[b, half, offsets[level] : offsets[level + 1]]
                if level > 0:
                    slot = wov.at[level - 1, half]
                    slot[pl.ds(0, tile // 2**level, stride=2**level), :] = rows
                    rows = slot[...]
                g_high, g_low = bf16_pair(rows)
                s = (1 - half) * tile
                g_sy[b, level, s : s + tile, :tile] = g_high
                g_sy[b, level, s : s + tile, tile:] = g_low
                g_high, g_low = bf16_pair(rows.T)
                s = half * tile
                g_an[b, level, s : s + tile, :tile] = g_high
                g_an[b, level, s : s + tile, tile:] = g_low

    own_copy.wait()
    arrivals = [(d, 1 - p if d == 1 else p) for p in range(2) for d in single]
    arrivals += [(d, p) for d in range(1, n_basis) if d not in single for p in range(2)]
    for d, p in arrivals:
        block_copies[d, p].wait_recv()
        for other in range(d + 1, n_basis):
            bit = (other & -other) if p == 0 else 1 << (other.bit_length() - 1)
            if other not in single and other ^ bit == d:
                block_copies[other, p].start()
        if (d, p) in halo_copies:
            halo_copies[d, p].start()

    for d in range(n_basis):
        for p in range(len(halo_halves)):
            halo_copies[d, p].wait_recv()
        x_high, x_low = bf16_pair(xg[peers[d]])
        for b in range(bases):
            wide = dot(a_lhs[b], x_high)
            z = wide[:used] + wide[used:] + dot(a_lhs[b, :used], x_low)
            high, low = bf16_pair(z)
            for part in range(per_block):
                at = peers[d] * per_block + part
                z_hi[b, at, :, :] = high[:, part * tile : (part + 1) * tile]
                z_lo[b, at, :, :] = low[:, part * tile : (part + 1) * tile]

    for copy in loads:
        copy.wait()
    lane = lax.broadcasted_iota(jnp.int32, (tile, tile), 1)
    row = lax.broadcasted_iota(jnp.int32, (tile, tile), 0)
    stores = []

    def windows(source, first, last, step):
        pieces = [source(j)[first:last] for j in range(tiles)]
        return jnp.concatenate(
            [
                jnp.concatenate(
                    [pieces[j], pieces[(j + 1) % tiles]] if step > 0 else [pieces[j - 1], pieces[j]], axis=1
                )
                for j in range(tiles)
            ],
            axis=0,
        )

    def columns(high_src, low_src, matrix, first, last, step):
        wide = dot(windows(high_src, first, last, step), matrix[...])
        return wide[:, :tile] + wide[:, tile:] + dot(windows(low_src, first, last, step), matrix[:, :tile])

    for b in range(bases):
        for level in range(LEVELS):
            y = columns(
                lambda j: z_hi[b, j], lambda j: z_lo[b, j], g_an.at[b, level],
                offsets[level], offsets[level + 1], 1,
            )
            stride, many = 2**level, tile // 2**level
            for j in range(tiles):
                mine = y[j * many : (j + 1) * many]
                slot = coef.at[j]
                if level == 0:
                    slot[...] = mine
                else:
                    held = slot[pl.ds(0, many, stride=stride), :]
                    slot[pl.ds(0, many, stride=stride), :] = jnp.where(
                        lane[:many] % stride == 0, mine, held
                    )
        for j in range(tiles):
            limit = thrv[b, j]
            dtile[b, j, :, :] = jnp.clip(dualv[b, j] + coef[j] * norm_scale, -limit, limit)
            copy = pltpu.make_async_copy(
                dtile.at[b, j], out_dual.at[b, :, pl.ds(j * tile, tile)], store_sem.at[b * tiles + j]
            )
            copy.start()
            stores.append(copy)
        for level in range(LEVELS):
            stride, many = 2**level, tile // 2**level
            highs, lows = [], []
            for j in range(tiles):
                slot = dtile.at[b, j]
                value = slot[...] if level == 0 else slot[pl.ds(0, many, stride=stride), :]
                if level < LEVELS - 1:
                    deeper = (row[:many] % 2 == 0) & (lane[:many] % (2 * stride) == 0)
                    value = jnp.where(deeper, 0.0, value)
                high, low = bf16_pair(value)
                highs.append(high)
                lows.append(low)
            e = columns(lambda j: highs[j], lambda j: lows[j], g_sy.at[b, level], 0, many, -1)
            e_high, e_low = bf16_pair(e)
            first = b * 2 * tile + offsets[level]
            for j in range(tiles):
                e_hi[j, first : first + many, :] = e_high[j * many : (j + 1) * many]
                e_lo[j, first : first + many, :] = e_low[j * many : (j + 1) * many]
        first = b * 2 * tile + used
        rest = 2 * tile - used
        for j in range(tiles):
            e_hi[j, first : first + rest, :] = jnp.zeros((rest, tile), jnp.bfloat16)
            e_lo[j, first : first + rest, :] = jnp.zeros((rest, tile), jnp.bfloat16)

    order = list(range(n_basis - 1, -1, -1))
    carry_copies, part_copies = {}, {}
    for d in order:
        at = peers[d]
        e_h = jnp.concatenate([e_hi[at * per_block + part] for part in range(per_block)], axis=1)
        e_l = jnp.concatenate([e_lo[at * per_block + part] for part in range(per_block)], axis=1)
        wide = dot(a_t[...], e_h)
        pbuf[d, :, :] = wide[: 2 * tile] + wide[2 * tile :] + dot(a_t[: 2 * tile], e_l)
        for p, (first, count) in enumerate(halo_halves):
            carry_copies[d, p] = remote(
                pbuf.at[d, pl.ds(tile + first, count)], hbuf.at[d, pl.ds(first, count)],
                ps_send.at[d, p], ps_recv.at[d, p], (after, me),
            )
            carry_copies[d, p].start()
    for d in order:
        for p, (first, count) in enumerate(halves):
            if (d, p) in carry_copies:
                rows = pl.ds(*halo_halves[p])
                carry_copies[d, p].wait_recv()
                pbuf[d, rows, :] = pbuf[d, rows, :] + hbuf[d, rows, :]
            if d > 0:
                part_copies[d, p] = remote(
                    pbuf.at[d, pl.ds(first, count)], rbuf.at[d, pl.ds(first, count)],
                    rs_send.at[d, p], rs_recv.at[d, p], (strip, peers[d]),
                )
                part_copies[d, p].start()
    total = pbuf[0, :tile, :]
    for d in order:
        if d > 0:
            for p in range(len(halves)):
                part_copies[d, p].wait_recv()
            total = total + rbuf[d]
    out_image[...] = total * norm_scale

    sent = (block_copies, halo_copies, carry_copies, part_copies)
    for copy in [copy for group in sent for copy in group.values()]:
        copy.wait_send()
    for copy in stores:
        copy.wait()


def solution(mesh):
    n_strip, n_basis = mesh.shape["strip"], mesh.shape["basis"]

    def on_device(sky_image, dual_coeffs, thresholds):
        bases, tile, cols = dual_coeffs.shape
        width = sky_image.shape[1]
        tiles = cols // tile
        reach = 2 * BASES - 2
        halo = -(-reach * (2**LEVELS - 1) // 8) * 8
        assert halo <= tile and width % tile == 0 and cols == width * n_basis
        assert n_basis & (n_basis - 1) == 0 and tile % 2**LEVELS == 0
        used = sum(tile // 2**level for level in range(LEVELS))
        f32, bf16 = jnp.float32, jnp.bfloat16
        dma = pltpu.SemaphoreType.DMA
        vmem, anywhere = pl.BlockSpec(memory_space=pltpu.VMEM), pl.BlockSpec(memory_space=pl.ANY)
        table = jnp.asarray(level_table(tile))
        return pl.pallas_call(
            functools.partial(kernel, (n_strip, n_basis, bases, tile, width, cols, halo)),
            out_shape=(
                jax.ShapeDtypeStruct(dual_coeffs.shape, f32),
                jax.ShapeDtypeStruct(sky_image.shape, f32),
            ),
            in_specs=[anywhere, anywhere, anywhere, anywhere],
            out_specs=(anywhere, vmem),
            scratch_shapes=[
                pltpu.VMEM((n_basis, 2 * tile, width), f32),
                pltpu.VMEM((bases, 2, 2 * tile, tile), f32),
                pltpu.VMEM((LEVELS - 1, 2, tile, tile), f32),
                pltpu.VMEM((bases, 2 * used, 2 * tile), bf16),
                pltpu.VMEM((4 * tile, bases * 2 * tile), bf16),
                pltpu.VMEM((bases, LEVELS, 2 * tile, 2 * tile), bf16),
                pltpu.VMEM((bases, LEVELS, 2 * tile, 2 * tile), bf16),
                pltpu.VMEM((bases, tiles, tile, tile), f32),
                pltpu.VMEM((bases, tiles, tile, tile), f32),
                pltpu.VMEM((bases, tiles, used, tile), bf16),
                pltpu.VMEM((bases, tiles, used, tile), bf16),
                pltpu.VMEM((tiles, tile, tile), f32),
                pltpu.VMEM((bases, tiles, tile, tile), f32),
                pltpu.VMEM((tiles, bases * 2 * tile, tile), bf16),
                pltpu.VMEM((tiles, bases * 2 * tile, tile), bf16),
                pltpu.VMEM((n_basis, 2 * tile, width), f32),
                pltpu.VMEM((n_basis, halo, width), f32),
                pltpu.VMEM((n_basis, tile, width), f32),
                dma((2 + 2 * tiles,)),
                dma((bases * tiles,)),
            ] + [dma((n_basis, 2)) for _ in range(8)],
            compiler_params=pltpu.CompilerParams(
                collective_id=0, has_side_effects=True, vmem_limit_bytes=67_043_328 - 1_400_000
            ),
        )(sky_image, table, dual_coeffs, thresholds)

    placed = (P("strip", "basis"), P("basis", "strip", None), P("basis", "strip", None))
    return jax.shard_map(
        on_device,
        mesh=mesh,
        in_specs=placed,
        out_specs=(P("basis", "strip", None), P("strip", "basis")),
        check_vma=False,
    )
```
